128 devices in a mesh: row: 16 (over y, z), col: 8 (over x, core).
Axes of the slice: x: 4, y: 4, z: 4, core: 2. Of those that a mesh axis runs over, the one named last changes fastest.
Arguments:
- grad_window: float32 [8192, 14336], P('row', 'col'), may hold values from -6 to 6
- rows_first: float32 [8192, 256], P('row'), may hold values from -0.0625 to 0.0625
- cols_first: float32 [14336, 256], P('col'), may hold values from -0.046875 to 0.046875
- rows_second: float32 [8192, 256], P('row'), may hold values from -0.0625 to 0.0625
- cols_second: float32 [14336, 256], P('col'), may hold values from -0.046875 to 0.046875
- inverse_first: float32 [256, 256], replicated, may hold values from -2 to 2, as said below
- inverse_second: float32 [256, 256], replicated, may hold values from -2 to 2, as said below
Outputs:
- panel_second: float32 [8192, 256], P('row')
- pivot_second: float32 [14336, 256], P('col')
- panel_first: float32 [8192, 256], P('row')
- pivot_first: float32 [14336, 256], P('col')
The draws below stay inside these ranges and needn't reach their ends.
Inputs may be any that keep to these rules, and one draw needn't show every extreme that they name: `inverse_first`: lower triangular, diagonal entries between 1 and 2. `inverse_second`: lower triangular, diagonal entries between 1 and 2.
All inputs are finite; a program needn't handle non-finite values.
Results may differ from the reference program's by a relative error of at most 0.000071.
Values sent between devices are 32-bit elements; how exact they have to be, the bound alone decides.
No kernel may reach another device: no remote copies, remote signals or barrier semaphores. Data moves between devices by JAX's collectives and lax.ppermute only.
A program may use at most 64 MiB of HBM per device.

```python
import jax
import jax.numpy as jnp
from jax import lax

NB = 256
R = 8192
C = 14336


def lower_inverse(key):
    first_key, second_key = jax.random.split(key)
    diagonal = jax.random.uniform(first_key, (NB,), jnp.float32, 1.0, 2.0)
    spread = jnp.clip(jax.random.normal(second_key, (NB, NB), jnp.float32), -4.0, 4.0) * (0.5 * NB ** (-0.5))
    return jnp.tril(spread, -1) + jnp.diag(diagonal)


def draw_inverse_first(key, part):
    return lower_inverse(jax.random.fold_in(key, 11))


def draw_inverse_second(key, part):
    return lower_inverse(jax.random.fold_in(key, 23))


def block_levels(rng, shape, shards, least, top_value):
    def one(position, blocks):
        steps = jax.random.uniform(jax.random.fold_in(jax.random.fold_in(rng, 6), position), (blocks,), jnp.float32, least / len(shards), top_value / len(shards))
        return jnp.repeat(jnp.exp(steps), shape[position] // blocks).reshape((-1,) + (1,) * (len(shape) - position - 1))

    gain = one(*shards[0])
    for cut in shards[1:]:
        gain = gain * one(*cut)
    return gain


def bell_draw(key, dims, scale, limit, pieces=(), dtype=jnp.bfloat16):
    entries = scale * jax.random.normal(key, dims, jnp.float32)
    if pieces:
        entries = entries * block_levels(key, dims, pieces, -0.22, 0.18)
    return jnp.clip(entries, -limit, limit).astype(dtype)


def setup_inputs(seed: int = 0) -> dict:
    keys = jax.random.split(jax.random.key(seed), 8)
    grad_window = bell_draw(keys[0], (R, C), 1.0, 6.0, ((0, 16), (1, 8)), jnp.float32)
    rows_first = bell_draw(keys[1], (R, NB), R ** -0.5, 0.0625, ((0, 16),), jnp.float32)
    cols_first = bell_draw(keys[2], (C, NB), C ** -0.5, 0.046875, ((0, 8),), jnp.float32)
    rows_second = bell_draw(keys[3], (R, NB), R ** -0.5, 0.0625, ((0, 16),), jnp.float32)
    cols_second = bell_draw(keys[4], (C, NB), C ** -0.5, 0.046875, ((0, 8),), jnp.float32)
    inverse_first = draw_inverse_first(jax.random.fold_in(keys[7], 71), 0)
    inverse_second = draw_inverse_second(jax.random.fold_in(keys[7], 71), 0)
    return dict(grad_window=grad_window, rows_first=rows_first, cols_first=cols_first, rows_second=rows_second, cols_second=cols_second, inverse_first=inverse_first, inverse_second=inverse_second)


def matmul(left, right):
    return jnp.dot(left, right, precision=lax.Precision.HIGHEST, preferred_element_type=jnp.float32)


def reference(grad_window, rows_first, cols_first, rows_second, cols_second, inverse_first, inverse_second):
    left_second = -matmul(grad_window, cols_second)
    panel_second = matmul(left_second, inverse_second)
    pivot_second = matmul(-matmul(grad_window.T, rows_second), inverse_second)
    grad_next = grad_window.at[:, C - NB:].add(panel_second)
    panel_first = matmul(-matmul(grad_next, cols_first), inverse_first)
    pivot_first = matmul(-matmul(grad_next.T, rows_first), inverse_first)
    return panel_second, pivot_second, panel_first, pivot_first
```

```python
import jax
import jax.numpy as jnp
from jax import lax
from jax.sharding import PartitionSpec as P

SIDE = 4


def matmul(left, right):
    return jnp.dot(left, right, precision=lax.Precision.HIGH, preferred_element_type=jnp.float32)


def tmatmul(left, right):
    return lax.dot_general(
        left,
        right,
        (((0,), (0,)), ((), ())),
        precision=lax.Precision.HIGH,
        preferred_element_type=jnp.float32,
    )


def row_pairs(dy, dz):
    return [
        (y * SIDE + z, ((y + dy) % SIDE) * SIDE + (z + dz) % SIDE)
        for y in range(SIDE)
        for z in range(SIDE)
    ]


def shift_y(value, step):
    return lax.ppermute(value, "row", row_pairs(step, 0))


def shift_z(value, step):
    return lax.ppermute(value, "row", row_pairs(0, step))


def shift_x(value, step):
    pairs = [(x * 2 + k, ((x + step) % SIDE) * 2 + k) for x in range(SIDE) for k in range(2)]
    return lax.ppermute(value, "col", pairs)


def swap_core(value):
    return lax.ppermute(value, "col", [(c, c ^ 1) for c in range(2 * SIDE)])


def block(value, index):
    return lax.dynamic_index_in_dim(value, index, 0, keepdims=False)


STEPS = (2, 1, 3)


def scatter_stage(parts):
    got = [[] for _ in parts]
    for step in STEPS:
        for i, (blocks, place, shift) in enumerate(parts):
            got[i].append(shift(block(blocks, (place + step) % SIDE), step))
    return [
        block(blocks, place) + got[i][0] + got[i][1] + got[i][2]
        for i, (blocks, place, _) in enumerate(parts)
    ]


def gather_stage(parts):
    out = [
        lax.dynamic_update_index_in_dim(jnp.zeros((SIDE,) + own.shape, own.dtype), own, place, 0)
        for own, place, _ in parts
    ]
    for step in STEPS:
        for i, (own, place, shift) in enumerate(parts):
            got = shift(own, step)
            out[i] = lax.dynamic_update_index_in_dim(out[i], got, (place - step) % SIDE, 0)
    return out


def row_sum(partial, y, z, finish):
    rows, width = partial.shape
    half, quarter, piece = rows // 2, rows // 8, rows // 32
    first = partial[:half].reshape(SIDE, quarter, width)
    second = partial[half:].reshape(SIDE, quarter, width)
    first, second = scatter_stage([(first, y, shift_y), (second, z, shift_z)])
    first, second = scatter_stage(
        [
            (first.reshape(SIDE, piece, width), z, shift_z),
            (second.reshape(SIDE, piece, width), y, shift_y),
        ]
    )
    done = finish(jnp.concatenate([first, second], 0))
    first, second = gather_stage([(done[:piece], z, shift_z), (done[piece:], y, shift_y)])
    first, second = gather_stage(
        [(first.reshape(quarter, width), y, shift_y), (second.reshape(quarter, width), z, shift_z)]
    )
    return jnp.concatenate([first.reshape(half, width), second.reshape(half, width)], 0)


def local(
    grad_window, rows_first, cols_first, rows_second, cols_second, inverse_first, inverse_second
):
    row = lax.axis_index("row")
    col = lax.axis_index("col")
    y, z = row // SIDE, row % SIDE
    x, core = col // 2, col % 2
    last = 2 * SIDE - 1
    is_last = col == last
    tile_cols = grad_window.shape[1]
    tile_rows = grad_window.shape[0]
    width = inverse_first.shape[0]

    tail = cols_first[tile_cols - width :]
    held = jnp.where(is_last, tail, 0.0)
    for target in (1, 5, 3):
        held = held + lax.ppermute(tail, "col", [(last, target)])
    other = lax.ppermute(held, "col", [(2 * i + 1, 2 * i) for i in range(SIDE)])
    tail = jnp.where(core == 1, held, other)

    left = matmul(grad_window, jnp.concatenate([cols_second, cols_first], 1))
    left = left.reshape(2, tile_rows // 2, 2 * width)
    left = block(left, core) + swap_core(block(left, 1 - core))
    (left,) = scatter_stage([(left.reshape(SIDE, tile_rows // 8, 2 * width), x, shift_x)])
    share_second = matmul(-left[:, :width], inverse_second)
    share_first = matmul(-(left[:, width:] + matmul(share_second, tail)), inverse_first)
    share = jnp.concatenate([share_second, share_first], 1)
    (half,) = gather_stage([(share, x, shift_x)])
    half = half.reshape(tile_rows // 2, 2 * width)
    both = jnp.stack([half, swap_core(half)])
    panels = jnp.concatenate([block(both, core), block(both, 1 - core)], 0)
    panel_second, panel_first = panels[:, :width], panels[:, width:]

    pivot_second = row_sum(
        tmatmul(grad_window, rows_second), y, z, lambda total: matmul(-total, inverse_second)
    )
    end = grad_window[:, tile_cols - width :] + jnp.where(is_last, panel_second, 0.0)
    partial = jnp.concatenate(
        [tmatmul(grad_window[:, : tile_cols - width], rows_first), tmatmul(end, rows_first)], 0
    )
    pivot_first = row_sum(partial, y, z, lambda total: matmul(-total, inverse_first))
    return (panel_second, pivot_second, panel_first, pivot_first)


def solution(mesh):
    in_specs = (
        P("row", "col"),
        P("row", None),
        P("col", None),
        P("row", None),
        P("col", None),
        P(),
        P(),
    )
    out_specs = (P("row", None), P("col", None), P("row", None), P("col", None))
    return jax.shard_map(local, mesh=mesh, in_specs=in_specs, out_specs=out_specs, check_vma=False)
```

```python
import jax
import jax.numpy as jnp
from jax import lax
from jax.sharding import PartitionSpec as P

SIDE = 4


def matmul(left, right):
    return jnp.dot(left, right, precision=lax.Precision.HIGH, preferred_element_type=jnp.float32)


def tmatmul(left, right):
    return lax.dot_general(
        left,
        right,
        (((0,), (0,)), ((), ())),
        precision=lax.Precision.HIGH,
        preferred_element_type=jnp.float32,
    )


def row_pairs(dy, dz):
    return [
        (y * SIDE + z, ((y + dy) % SIDE) * SIDE + (z + dz) % SIDE)
        for y in range(SIDE)
        for z in range(SIDE)
    ]


def shift_y(value, step):
    return lax.ppermute(value, "row", row_pairs(step, 0))


def shift_z(value, step):
    return lax.ppermute(value, "row", row_pairs(0, step))


def block(value, index):
    return lax.dynamic_index_in_dim(value, index, 0, keepdims=False)


STEPS = (2, 1, 3)


def scatter_stage(parts):
    got = [[] for _ in parts]
    for step in STEPS:
        for i, (blocks, place, shift) in enumerate(parts):
            got[i].append(shift(block(blocks, (place + step) % SIDE), step))
    return [
        block(blocks, place) + got[i][0] + got[i][1] + got[i][2]
        for i, (blocks, place, _) in enumerate(parts)
    ]


def sum_stage(parts):
    got = [[] for _ in parts]
    for step in STEPS:
        for i, (own, shift) in enumerate(parts):
            got[i].append(shift(own, step))
    return [own + got[i][0] + got[i][1] + got[i][2] for i, (own, _) in enumerate(parts)]


def local(
    grad_window, rows_first, cols_first, rows_second, cols_second, inverse_first, inverse_second
):
    row = lax.axis_index("row")
    col = lax.axis_index("col")
    y, z = row // SIDE, row % SIDE
    core = col % 2
    last = 2 * SIDE - 1
    is_last = col == last
    tile_rows, tile_cols = grad_window.shape
    width = inverse_first.shape[0]

    left = matmul(grad_window, jnp.concatenate([cols_second, cols_first], 1))
    tail = jnp.where(is_last, cols_first[tile_cols - width :], 0.0)
    load = jnp.concatenate(
        [left, jnp.concatenate([tail[: width // 2], tail[width // 2 :]], 1)], 0
    )
    share = lax.psum_scatter(load, "col", scatter_dimension=0, tiled=True)
    full = lax.all_gather(share, "col", axis=0, tiled=True)
    tail = jnp.concatenate([full[tile_rows:, :width], full[tile_rows:, width:]], 0)
    panel_second = matmul(-full[:tile_rows, :width], inverse_second)
    panel_first = matmul(-(full[:tile_rows, width:] + matmul(panel_second, tail)), inverse_first)

    cross = tmatmul(matmul(-left[:, :width], inverse_second), rows_first)
    cross = cross + lax.ppermute(cross, "col", [(2 * i, 2 * i + 1) for i in range(SIDE)])
    others = [lax.ppermute(cross, "col", [(source, last)]) for source in (3, 1, 5)]
    cross = jnp.where(is_last, cross + others[0] + others[1] + others[2], 0.0)

    rows_both = jnp.concatenate([rows_second, rows_first], 1)
    half = tile_cols // 2
    quarter = half // SIDE
    first = tmatmul(grad_window[:, :half], rows_both)
    second = tmatmul(grad_window[:, half:], rows_both)
    second = second.at[half - width :, width:].add(cross)
    first, second = scatter_stage(
        [
            (first.reshape(SIDE, quarter, 2 * width), y, shift_y),
            (second.reshape(SIDE, quarter, 2 * width), z, shift_z),
        ]
    )
    first, second = sum_stage([(first, shift_z), (second, shift_y)])
    done = [
        jnp.concatenate(
            [matmul(-total[:, :width], inverse_second), matmul(-total[:, width:], inverse_first)], 1
        )
        for total in (first, second)
    ]
    pivots = [jnp.zeros((2 * SIDE, quarter, width), jnp.float32) for _ in range(2)]

    def place(value, index):
        for i in range(2):
            pivots[i] = lax.dynamic_update_index_in_dim(
                pivots[i], value[:, i * width : (i + 1) * width], index, 0
            )

    place(done[0], y)
    place(done[1], SIDE + z)
    for step in STEPS:
        place(shift_y(done[0], step), (y - step) % SIDE)
        place(shift_z(done[1], step), SIDE + (z - step) % SIDE)
    pivot_second, pivot_first = (value.reshape(tile_cols, width) for value in pivots)
    return (panel_second, pivot_second, panel_first, pivot_first)


def solution(mesh):
    in_specs = (
        P("row", "col"),
        P("row", None),
        P("col", None),
        P("row", None),
        P("col", None),
        P(),
        P(),
    )
    out_specs = (P("row", None), P("col", None), P("row", None), P("col", None))
    return jax.shard_map(local, mesh=mesh, in_specs=in_specs, out_specs=out_specs, check_vma=False)
```

```python
import jax
import jax.numpy as jnp
from jax import lax
from jax.experimental import pallas as pl
from jax.experimental.pallas import tpu as pltpu
from jax.sharding import PartitionSpec as P

SIDE = 4
STEPS = (2, 1, 3)


def matmul(left, right):
    return jnp.dot(left, right, precision=lax.Precision.HIGH, preferred_element_type=jnp.float32)


def pairs(step, swap):
    out = []
    for y in range(SIDE):
        for z in range(SIDE):
            for x in range(SIDE):
                for core in range(2):
                    if core == swap:
                        to_y, to_z = (y + step) % SIDE, z
                    else:
                        to_y, to_z = y, (z + step) % SIDE
                    out.append(
                        (
                            (y * SIDE + z) * 2 * SIDE + 2 * x + core,
                            (to_y * SIDE + to_z) * 2 * SIDE + 2 * x + core,
                        )
                    )
    return out


def shift(value, step, swap):
    return lax.ppermute(value, ("row", "col"), pairs(step, swap))


def block(value, index):
    return lax.dynamic_index_in_dim(value, index, 0, keepdims=False)


def split(value):
    high = value.astype(jnp.bfloat16)
    return high, (value - high.astype(jnp.float32)).astype(jnp.bfloat16)


def dot3(left, right):
    total = jnp.dot(left[0], right[1], preferred_element_type=jnp.float32)
    total += jnp.dot(left[1], right[0], preferred_element_type=jnp.float32)
    return total + jnp.dot(left[0], right[0], preferred_element_type=jnp.float32)


def tdot3(left, right):
    def product(a, b):
        return lax.dot_general(a, b, (((0,), (0,)), ((), ())), preferred_element_type=jnp.float32)

    return product(left[0], right[1]) + product(left[1], right[0]) + product(left[0], right[0])


def whole(shape):
    return pl.BlockSpec(shape, lambda i: (0,) * len(shape))


def panel_kernel(full_ref, second_ref, first_ref, panel_second_ref, panel_first_ref):
    rows = panel_second_ref.shape[0]
    panel = dot3(split(-full_ref[:rows]), split(second_ref[...]))
    panel_second_ref[...] = panel
    left = full_ref[rows : 2 * rows] + dot3(split(panel), split(full_ref[2 * rows :]))
    panel_first_ref[...] = dot3(split(-left), split(first_ref[...]))


def panels(full, inverse_second, inverse_first):
    width = inverse_first.shape[0]
    rows = (full.shape[0] - width) // 2
    shape = jax.ShapeDtypeStruct((rows, width), jnp.float32)
    return pl.pallas_call(
        panel_kernel,
        grid=(1,),
        in_specs=[whole(full.shape), whole((width, width)), whole((width, width))],
        out_specs=[whole((rows, width))] * 2,
        out_shape=[shape, shape],
        cost_estimate=pl.CostEstimate(
            flops=18 * rows * width * width, bytes_accessed=16 * rows * width, transcendentals=0
        ),
        name="panels",
    )(full, inverse_second, inverse_first)


def place_of(row, col):
    return jnp.where(lax.rem(col, 2) == 0, lax.div(row, SIDE), lax.rem(row, SIDE))


def products_kernel(
    window_hbm, cols_second_hbm, cols_first_hbm, rows_second_hbm, rows_first_hbm, inverse_hbm,
    load_hbm, cross_hbm, *refs,
):
    outs, refs = refs[:SIDE], refs[SIDE:]
    (window, cols, rows, inverse, left, tail, pivot, cross, high, low, sem_in, sem_chunk, sem_out,
     sem_pivot) = refs
    chunks, tile_rows, width = window.shape
    piece = width // SIDE
    halves = (slice(0, width), slice(width, 2 * width))

    ready = [
        pltpu.make_async_copy(rows_second_hbm, rows.at[:, halves[0]], sem_in.at[0]),
        pltpu.make_async_copy(rows_first_hbm, rows.at[:, halves[1]], sem_in.at[1]),
        pltpu.make_async_copy(inverse_hbm, inverse, sem_in.at[2]),
    ]
    arriving = []
    for j in range(chunks):
        at = pl.ds(j * width, width)
        arriving.append(
            [
                pltpu.make_async_copy(window_hbm.at[:, at], window.at[j], sem_chunk.at[j, 0]),
                pltpu.make_async_copy(
                    cols_second_hbm.at[at], cols.at[j, :, halves[0]], sem_chunk.at[j, 1]
                ),
                pltpu.make_async_copy(
                    cols_first_hbm.at[at], cols.at[j, :, halves[1]], sem_chunk.at[j, 2]
                ),
            ]
        )
    for copy in ready[:2] + [copy for group in arriving for copy in group] + ready[2:]:
        copy.start()

    place = place_of(lax.axis_index("row"), lax.axis_index("col"))
    leaving = []
    for copy in ready[:2]:
        copy.wait()
    high[...], low[...] = split(rows[...])
    for j in range(chunks):
        for copy in arriving[j]:
            copy.wait()
        part = split(window[j])
        product = dot3(part, split(cols[j]))
        if j == 0:
            left[...] = product
        else:
            left[...] += product
        pivot[j] = tdot3(part, (high[...], low[...]))
        for step in range(SIDE):
            start = pl.multiple_of(lax.rem(place + step, SIDE) * piece, piece)
            for i in range(2):
                copy = pltpu.make_async_copy(
                    pivot.at[j, pl.ds(start, piece), halves[i]],
                    outs[step].at[pl.ds((i * chunks + j) * piece, piece)],
                    sem_pivot.at[j, i * SIDE + step],
                )
                copy.start()
                leaving.append(copy)

    is_last = lax.axis_index("col") == 2 * SIDE - 1
    tail[...] = jnp.where(is_last, cols[chunks - 1, :, halves[1]], 0.0)
    for i, source in enumerate((left.at[:, halves[0]], left.at[:, halves[1]], tail)):
        copy = pltpu.make_async_copy(
            source, load_hbm.at[pl.ds(i * tile_rows, source.shape[0])], sem_out.at[i]
        )
        copy.start()
        leaving.append(copy)
    ready[2].wait()
    panel = dot3(split(left[:, halves[0]]), split(inverse[...]))
    cross[...] = tdot3(split(-panel), (high[:, halves[1]], low[:, halves[1]]))
    copy = pltpu.make_async_copy(cross, cross_hbm, sem_out.at[3])
    copy.start()
    for copy in leaving + [copy]:
        copy.wait()


def products(window, cols_second, cols_first, rows_second, rows_first, inverse):
    tile_rows, tile_cols = window.shape
    width = inverse.shape[0]
    chunks = tile_cols // width
    hbm = pl.BlockSpec(memory_space=pl.ANY)
    f32 = lambda *shape: jax.ShapeDtypeStruct(shape, jnp.float32)
    buffer = lambda *shape: pltpu.VMEM(shape, jnp.float32)
    return pl.pallas_call(
        products_kernel,
        in_specs=[hbm] * 6,
        out_specs=[hbm] * (2 + SIDE),
        out_shape=[f32(2 * tile_rows + width, width), f32(width, width)]
        + [f32(2 * tile_cols // SIDE, width)] * SIDE,
        scratch_shapes=[
            buffer(chunks, tile_rows, width),
            buffer(chunks, width, 2 * width),
            buffer(tile_rows, 2 * width),
            buffer(width, width),
            buffer(tile_rows, 2 * width),
            buffer(width, width),
            buffer(chunks, width, 2 * width),
            buffer(width, width),
            pltpu.VMEM((tile_rows, 2 * width), jnp.bfloat16),
            pltpu.VMEM((tile_rows, 2 * width), jnp.bfloat16),
            pltpu.SemaphoreType.DMA((3,)),
            pltpu.SemaphoreType.DMA((chunks, 3)),
            pltpu.SemaphoreType.DMA((4,)),
            pltpu.SemaphoreType.DMA((chunks, 2 * SIDE)),
        ],
        cost_estimate=pl.CostEstimate(
            flops=24 * tile_rows * tile_cols * width,
            bytes_accessed=4 * (tile_rows * tile_cols + 4 * tile_cols * width),
            transcendentals=0,
        ),
        name="products",
    )(window, cols_second, cols_first, rows_second, rows_first, inverse)


def after(value, *others):
    return lax.optimization_barrier((value,) + others)[0]


def local(
    grad_window, rows_first, cols_first, rows_second, cols_second, inverse_first, inverse_second
):
    row = lax.axis_index("row")
    col = lax.axis_index("col")
    last = 2 * SIDE - 1
    is_last = col == last
    tile_cols = grad_window.shape[1]
    width = inverse_first.shape[0]
    chunks, piece = tile_cols // width, width // SIDE
    place = place_of(row, col)

    load, cross, *blocks = products(
        grad_window, cols_second, cols_first, rows_second, rows_first, inverse_second
    )

    share = lax.psum_scatter(load, "col", scatter_dimension=0, tiled=True)

    cross = cross + lax.ppermute(cross, "col", [(2 * i, 2 * i + 1) for i in range(SIDE)])
    others = [lax.ppermute(cross, "col", [(source, last)]) for source in (3, 1, 5)]
    cross = jnp.where(is_last, cross + others[0] + others[1] + others[2], 0.0)
    late = cross.reshape(SIDE, piece, width)
    late = [block(late, (place + step) % SIDE) for step in range(SIDE)]

    def arrivals(values, swap):
        return [shift(values[step], step, swap) for step in STEPS]

    got = arrivals(blocks, 0)
    got_late = arrivals(late, 0)
    value = blocks[0] + got[0] + got[1] + got[2]
    late = late[0] + got_late[0] + got_late[1] + got_late[2]
    value = value.at[value.shape[0] - piece :].add(late)

    got = arrivals([value] * SIDE, 1)
    full = lax.all_gather(after(share, got[0]), "col", axis=0, tiled=True)
    panel_second, panel_first = panels(full, inverse_second, inverse_first)
    value = value + got[0] + got[1] + got[2]

    half = value.shape[0] // 2
    value = jnp.concatenate(
        [matmul(-value[:half], inverse_second), matmul(-value[half:], inverse_first)], 0
    )
    got = arrivals([value] * SIDE, 0)
    pivots = [jnp.zeros((chunks, SIDE, piece, width), jnp.float32)] * 2
    parts = [(value, 0)] + list(zip(got, STEPS))
    for i, (part, step) in enumerate(parts):
        if i == len(parts) - 2:
            pivots = after(pivots, panel_second, panel_first)
        pivots = [
            lax.dynamic_update_index_in_dim(
                pivot, rows.reshape(chunks, piece, width), (place - step) % SIDE, 1
            )
            for pivot, rows in zip(pivots, (part[:half], part[half:]))
        ]
    pivot_second, pivot_first = (pivot.reshape(tile_cols, width) for pivot in pivots)
    return (panel_second, pivot_second, panel_first, pivot_first)


def solution(mesh):
    in_specs = (
        P("row", "col"),
        P("row", None),
        P("col", None),
        P("row", None),
        P("col", None),
        P(),
        P(),
    )
    out_specs = (P("row", None), P("col", None), P("row", None), P("col", None))
    return jax.shard_map(local, mesh=mesh, in_specs=in_specs, out_specs=out_specs, check_vma=False)
```

```python
import jax
import jax.numpy as jnp
from jax import lax
from jax.experimental import pallas as pl
from jax.experimental.pallas import tpu as pltpu
from jax.sharding import PartitionSpec as P

SIDE = 4
STEPS = (2, 1, 3)


def matmul(left, right):
    return jnp.dot(left, right, precision=lax.Precision.HIGH, preferred_element_type=jnp.float32)


def pairs(step, swap):
    out = []
    for y in range(SIDE):
        for z in range(SIDE):
            for x in range(SIDE):
                for core in range(2):
                    if core == swap:
                        to_y, to_z = (y + step) % SIDE, z
                    else:
                        to_y, to_z = y, (z + step) % SIDE
                    out.append(
                        (
                            (y * SIDE + z) * 2 * SIDE + 2 * x + core,
                            (to_y * SIDE + to_z) * 2 * SIDE + 2 * x + core,
                        )
                    )
    return out


def shift(value, step, swap):
    return lax.ppermute(value, ("row", "col"), pairs(step, swap))


def shift_x(value, step):
    pairs = [(2 * x + k, 2 * ((x + step) % SIDE) + k) for x in range(SIDE) for k in range(2)]
    return lax.ppermute(value, "col", pairs)


def swap_core(value):
    return lax.ppermute(value, "col", [(i, i ^ 1) for i in range(2 * SIDE)])


def block(value, index):
    return lax.dynamic_index_in_dim(value, index, 0, keepdims=False)


def split(value):
    high = value.astype(jnp.bfloat16)
    return high, (value - high.astype(jnp.float32)).astype(jnp.bfloat16)


def dot3(left, right):
    total = jnp.dot(left[0], right[1], preferred_element_type=jnp.float32)
    total += jnp.dot(left[1], right[0], preferred_element_type=jnp.float32)
    return total + jnp.dot(left[0], right[0], preferred_element_type=jnp.float32)


def tdot3(left, right):
    def product(a, b):
        return lax.dot_general(a, b, (((0,), (0,)), ((), ())), preferred_element_type=jnp.float32)

    return product(left[0], right[1]) + product(left[1], right[0]) + product(left[0], right[0])


def place_of(row, col):
    return jnp.where(lax.rem(col, 2) == 0, lax.div(row, SIDE), lax.rem(row, SIDE))


def pivot_kernel(window_hbm, rows_second_hbm, rows_first_hbm, *refs):
    outs, refs = refs[:SIDE], refs[SIDE:]
    window, rows, pivot, high, low, sem_rows, sem_window, sem_out = refs
    chunks, _, width = window.shape
    piece = width // SIDE
    halves = (slice(0, width), slice(width, 2 * width))

    ready = [
        pltpu.make_async_copy(source, rows.at[:, halves[i]], sem_rows.at[i])
        for i, source in enumerate((rows_second_hbm, rows_first_hbm))
    ]
    arriving = [
        pltpu.make_async_copy(
            window_hbm.at[:, pl.ds(j * width, width)], window.at[j], sem_window.at[j]
        )
        for j in range(chunks)
    ]
    for copy in ready + arriving:
        copy.start()
    place = place_of(lax.axis_index("row"), lax.axis_index("col"))
    leaving = []
    for copy in ready:
        copy.wait()
    high[...], low[...] = split(rows[...])
    for j in range(chunks):
        arriving[j].wait()
        pivot[j] = tdot3(split(window[j]), (high[...], low[...]))
        for step in range(SIDE):
            start = pl.multiple_of(lax.rem(place + step, SIDE) * piece, piece)
            for i in range(2):
                copy = pltpu.make_async_copy(
                    pivot.at[j, pl.ds(start, piece), halves[i]],
                    outs[step].at[pl.ds((i * chunks + j) * piece, piece)],
                    sem_out.at[j, i * SIDE + step],
                )
                copy.start()
                leaving.append(copy)
    for copy in leaving:
        copy.wait()


def pivot_products(window, rows_second, rows_first):
    tile_rows, tile_cols = window.shape
    width = rows_first.shape[1]
    chunks = tile_cols // width
    hbm = pl.BlockSpec(memory_space=pl.ANY)
    buffer = lambda *shape: pltpu.VMEM(shape, jnp.float32)
    return pl.pallas_call(
        pivot_kernel,
        in_specs=[hbm] * 3,
        out_specs=[hbm] * SIDE,
        out_shape=[jax.ShapeDtypeStruct((2 * tile_cols // SIDE, width), jnp.float32)] * SIDE,
        scratch_shapes=[
            buffer(chunks, tile_rows, width),
            buffer(tile_rows, 2 * width),
            buffer(chunks, width, 2 * width),
            pltpu.VMEM((tile_rows, 2 * width), jnp.bfloat16),
            pltpu.VMEM((tile_rows, 2 * width), jnp.bfloat16),
            pltpu.SemaphoreType.DMA((2,)),
            pltpu.SemaphoreType.DMA((chunks,)),
            pltpu.SemaphoreType.DMA((chunks, 2 * SIDE)),
        ],
        cost_estimate=pl.CostEstimate(
            flops=12 * tile_rows * tile_cols * width,
            bytes_accessed=4 * (tile_rows * tile_cols + 2 * tile_cols * width),
            transcendentals=0,
        ),
        name="pivot_products",
    )(window, rows_second, rows_first)


def left_kernel(
    window_hbm, cols_second_hbm, cols_first_hbm, rows_hbm, inverse_hbm, own_hbm, other_hbm,
    cross_hbm, window, cols, rows, inverse, left, cross, sem_in, sem_chunk, sem_out,
):
    chunks, tile_rows, width = window.shape
    halves = (slice(0, width), slice(width, 2 * width))
    arriving = []
    for j in range(chunks):
        at = pl.ds(j * width, width)
        arriving.append(
            [
                pltpu.make_async_copy(window_hbm.at[:, at], window.at[j], sem_chunk.at[j, 0]),
                pltpu.make_async_copy(
                    cols_second_hbm.at[at], cols.at[j, :, halves[0]], sem_chunk.at[j, 1]
                ),
                pltpu.make_async_copy(
                    cols_first_hbm.at[at], cols.at[j, :, halves[1]], sem_chunk.at[j, 2]
                ),
            ]
        )
    ready = [
        pltpu.make_async_copy(rows_hbm, rows, sem_in.at[0]),
        pltpu.make_async_copy(inverse_hbm, inverse, sem_in.at[1]),
    ]
    for copy in [copy for group in arriving for copy in group] + ready:
        copy.start()
    for j in range(chunks):
        for copy in arriving[j]:
            copy.wait()
        product = dot3(split(window[j]), split(cols[j]))
        if j == 0:
            left[...] = product
        else:
            left[...] += product
    half = tile_rows // 2
    core = lax.rem(lax.axis_index("col"), 2)
    leaving = [
        pltpu.make_async_copy(
            left.at[pl.ds(pl.multiple_of(place * half, half), half)], target, sem_out.at[i]
        )
        for i, (place, target) in enumerate(((core, own_hbm), (1 - core, other_hbm)))
    ]
    for copy in leaving:
        copy.start()
    for copy in ready:
        copy.wait()
    panel = dot3(split(left[:, halves[0]]), split(inverse[...]))
    cross[...] = tdot3(split(-panel), split(rows[...]))
    leaving.append(pltpu.make_async_copy(cross, cross_hbm, sem_out.at[2]))
    leaving[-1].start()
    for copy in leaving:
        copy.wait()


def left_products(window, cols_second, cols_first, rows, inverse):
    tile_rows, tile_cols = window.shape
    width = inverse.shape[0]
    chunks = tile_cols // width
    hbm = pl.BlockSpec(memory_space=pl.ANY)
    f32 = lambda *shape: jax.ShapeDtypeStruct(shape, jnp.float32)
    buffer = lambda *shape: pltpu.VMEM(shape, jnp.float32)
    return pl.pallas_call(
        left_kernel,
        in_specs=[hbm] * 5,
        out_specs=[hbm] * 3,
        out_shape=[f32(tile_rows // 2, 2 * width)] * 2 + [f32(width, width)],
        scratch_shapes=[
            buffer(chunks, tile_rows, width),
            buffer(chunks, width, 2 * width),
            buffer(tile_rows, width),
            buffer(width, width),
            buffer(tile_rows, 2 * width),
            buffer(width, width),
            pltpu.SemaphoreType.DMA((2,)),
            pltpu.SemaphoreType.DMA((chunks, 3)),
            pltpu.SemaphoreType.DMA((3,)),
        ],
        cost_estimate=pl.CostEstimate(
            flops=12 * tile_rows * tile_cols * width,
            bytes_accessed=4 * (tile_rows * tile_cols + 2 * tile_cols * width),
            transcendentals=0,
        ),
        name="left_products",
    )(window, cols_second, cols_first, rows, inverse)


def after(value, *others):
    return lax.optimization_barrier((value,) + others)[0]


def local(
    grad_window, rows_first, cols_first, rows_second, cols_second, inverse_first, inverse_second
):
    row = lax.axis_index("row")
    col = lax.axis_index("col")
    last = 2 * SIDE - 1
    is_last = col == last
    tile_cols = grad_window.shape[1]
    width = inverse_first.shape[0]
    chunks, piece = tile_cols // width, width // SIDE
    place = place_of(row, col)

    far_place = place_of(row, col + 1)
    x, core = col // 2, col % 2

    own_left, other_left, cross = left_products(
        grad_window, cols_second, cols_first, rows_first, inverse_second
    )
    blocks = pivot_products(after(grad_window, cross), rows_second, rows_first)
    left = own_left + swap_core(other_left)

    cross = cross + lax.ppermute(cross, "col", [(2 * i, 2 * i + 1) for i in range(SIDE)])
    others = [lax.ppermute(cross, "col", [(source, last)]) for source in (3, 1, 5)]
    cross = jnp.where(is_last, cross + others[0] + others[1] + others[2], 0.0)
    late = cross.reshape(SIDE, piece, width)
    late = [block(late, (place + step) % SIDE) for step in range(SIDE)]

    def arrivals(values, swap):
        return [shift(values[step], step, swap) for step in STEPS]

    tail = cols_first[tile_cols - width :]
    held = jnp.where(is_last, tail, 0.0)
    for target in (1, 5, 3):
        held = held + lax.ppermute(after(tail, late[1]), "col", [(last, target)])

    tail = lax.ppermute(held, "col", [(2 * i + 1, 2 * i) for i in range(SIDE)])
    tail = jnp.where(core == 1, held, tail)
    left = after(left, late[1]).reshape(SIDE, -1, 2 * width)
    got_left = [shift_x(block(left, (x + step) % SIDE), step) for step in STEPS]
    left = block(left, x) + got_left[0] + got_left[1] + got_left[2]
    panel_second = matmul(-left[:, :width], inverse_second)
    panel_first = matmul(-(left[:, width:] + matmul(panel_second, tail)), inverse_first)
    panel = jnp.concatenate([panel_second, panel_first], 1)

    got = arrivals(blocks, 0)
    got_late = arrivals(late, 0)
    value = blocks[0] + got[0] + got[1] + got[2]
    late = late[0] + got_late[0] + got_late[1] + got_late[2]
    value = value.at[value.shape[0] - piece :].add(late)

    half = value.shape[0] // 2
    quarters = value.reshape(SIDE, half // 2, width)
    got = arrivals([block(quarters, (far_place + step) % SIDE) for step in range(SIDE)], 1)
    quarter = block(quarters, far_place) + got[0] + got[1] + got[2]
    inverse = jnp.where(far_place < SIDE // 2, inverse_second, inverse_first)
    quarter = matmul(-quarter, inverse)

    got = arrivals([quarter] * SIDE, 1)
    value = jnp.zeros((SIDE,) + quarter.shape, jnp.float32)
    for part, step in [(quarter, 0)] + list(zip(got, STEPS)):
        value = lax.dynamic_update_index_in_dim(value, part, (far_place - step) % SIDE, 0)
    value = value.reshape(2 * half, width)

    got = arrivals([value] * SIDE, 0)
    panel = after(panel, got[0])
    panels = jnp.zeros((SIDE,) + panel.shape, jnp.float32)
    for part, step in [(panel, 0)] + [(shift_x(panel, step), step) for step in STEPS]:
        panels = lax.dynamic_update_index_in_dim(panels, part, (x - step) % SIDE, 0)
    panels = panels.reshape(-1, 2 * width)
    both = jnp.zeros((2,) + panels.shape, jnp.float32)
    both = lax.dynamic_update_index_in_dim(both, panels, core, 0)
    both = lax.dynamic_update_index_in_dim(both, swap_core(panels), 1 - core, 0)
    both = both.reshape(-1, 2 * width)
    panel_second, panel_first = both[:, :width], both[:, width:]
    pivots = [jnp.zeros((chunks, SIDE, piece, width), jnp.float32)] * 2
    parts = [(value, 0)] + list(zip(got, STEPS))
    for i, (part, step) in enumerate(parts):
        if i == 1:
            pivots = after(pivots, panel_second, panel_first)
        pivots = [
            lax.dynamic_update_index_in_dim(
                pivot, rows.reshape(chunks, piece, width), (place - step) % SIDE, 1
            )
            for pivot, rows in zip(pivots, (part[:half], part[half:]))
        ]
    pivot_second, pivot_first = (pivot.reshape(tile_cols, width) for pivot in pivots)
    return (panel_second, pivot_second, panel_first, pivot_first)


def solution(mesh):
    in_specs = (
        P("row", "col"),
        P("row", None),
        P("col", None),
        P("row", None),
        P("col", None),
        P(),
        P(),
    )
    out_specs = (P("row", None), P("col", None), P("row", None), P("col", None))
    return jax.shard_map(local, mesh=mesh, in_specs=in_specs, out_specs=out_specs, check_vma=False)
```

```python
import jax
import jax.numpy as jnp
from jax import lax
from jax.experimental import pallas as pl
from jax.experimental.pallas import tpu as pltpu
from jax.sharding import PartitionSpec as P

SIDE = 4
STEPS = (2, 1, 3)


def matmul(left, right):
    return jnp.dot(left, right, precision=lax.Precision.HIGH, preferred_element_type=jnp.float32)


def pairs(step, swap):
    out = []
    for y in range(SIDE):
        for z in range(SIDE):
            for x in range(SIDE):
                for core in range(2):
                    if core == swap:
                        to_y, to_z = (y + step) % SIDE, z
                    else:
                        to_y, to_z = y, (z + step) % SIDE
                    out.append(
                        (
                            (y * SIDE + z) * 2 * SIDE + 2 * x + core,
                            (to_y * SIDE + to_z) * 2 * SIDE + 2 * x + core,
                        )
                    )
    return out


def shift(value, step, swap):
    return lax.ppermute(value, ("row", "col"), pairs(step, swap))


def shift_x(value, step):
    pairs = [(2 * x + k, 2 * ((x + step) % SIDE) + k) for x in range(SIDE) for k in range(2)]
    return lax.ppermute(value, "col", pairs)


def swap_core(value):
    return lax.ppermute(value, "col", [(i, i ^ 1) for i in range(2 * SIDE)])


def block(value, index):
    return lax.dynamic_index_in_dim(value, index, 0, keepdims=False)


def split(value):
    high = value.astype(jnp.bfloat16)
    return high, (value - high.astype(jnp.float32)).astype(jnp.bfloat16)


def dot3(left, right):
    total = jnp.dot(left[0], right[1], preferred_element_type=jnp.float32)
    total += jnp.dot(left[1], right[0], preferred_element_type=jnp.float32)
    return total + jnp.dot(left[0], right[0], preferred_element_type=jnp.float32)


def tdot3(left, right):
    def product(a, b):
        return lax.dot_general(a, b, (((0,), (0,)), ((), ())), preferred_element_type=jnp.float32)

    return product(left[0], right[1]) + product(left[1], right[0]) + product(left[0], right[0])


def place_of(row, col):
    return jnp.where(lax.rem(col, 2) == 0, lax.div(row, SIDE), lax.rem(row, SIDE))


def pivot_kernel(window_hbm, rows_second_hbm, rows_first_hbm, *refs):
    outs, refs = refs[:SIDE], refs[SIDE:]
    window, rows, pivot, high, low, sem_rows, sem_window, sem_out = refs
    chunks, _, width = window.shape
    piece = width // SIDE
    halves = (slice(0, width), slice(width, 2 * width))

    ready = [
        pltpu.make_async_copy(source, rows.at[:, halves[i]], sem_rows.at[i])
        for i, source in enumerate((rows_second_hbm, rows_first_hbm))
    ]
    arriving = [
        pltpu.make_async_copy(
            window_hbm.at[:, pl.ds(j * width, width)], window.at[j], sem_window.at[j]
        )
        for j in range(chunks)
    ]
    for copy in ready + arriving:
        copy.start()
    place = place_of(lax.axis_index("row"), lax.axis_index("col"))
    leaving = []
    for copy in ready:
        copy.wait()
    high[...], low[...] = split(rows[...])
    for j in range(chunks):
        arriving[j].wait()
        pivot[j] = tdot3(split(window[j]), (high[...], low[...]))
        for step in range(SIDE):
            start = pl.multiple_of(lax.rem(place + step, SIDE) * piece, piece)
            for i in range(2):
                copy = pltpu.make_async_copy(
                    pivot.at[j, pl.ds(start, piece), halves[i]],
                    outs[step].at[pl.ds((i * chunks + j) * piece, piece)],
                    sem_out.at[j, i * SIDE + step],
                )
                copy.start()
                leaving.append(copy)
    for copy in leaving:
        copy.wait()


def pivot_products(window, rows_second, rows_first):
    tile_rows, tile_cols = window.shape
    width = rows_first.shape[1]
    chunks = tile_cols // width
    hbm = pl.BlockSpec(memory_space=pl.ANY)
    buffer = lambda *shape: pltpu.VMEM(shape, jnp.float32)
    return pl.pallas_call(
        pivot_kernel,
        in_specs=[hbm] * 3,
        out_specs=[hbm] * SIDE,
        out_shape=[jax.ShapeDtypeStruct((2 * tile_cols // SIDE, width), jnp.float32)] * SIDE,
        scratch_shapes=[
            buffer(chunks, tile_rows, width),
            buffer(tile_rows, 2 * width),
            buffer(chunks, width, 2 * width),
            pltpu.VMEM((tile_rows, 2 * width), jnp.bfloat16),
            pltpu.VMEM((tile_rows, 2 * width), jnp.bfloat16),
            pltpu.SemaphoreType.DMA((2,)),
            pltpu.SemaphoreType.DMA((chunks,)),
            pltpu.SemaphoreType.DMA((chunks, 2 * SIDE)),
        ],
        cost_estimate=pl.CostEstimate(
            flops=12 * tile_rows * tile_cols * width,
            bytes_accessed=4 * (tile_rows * tile_cols + 2 * tile_cols * width),
            transcendentals=0,
        ),
        name="pivot_products",
    )(window, rows_second, rows_first)


def left_kernel(
    window_hbm, cols_second_hbm, cols_first_hbm, rows_hbm, inverse_hbm, own_hbm, other_hbm,
    cross_hbm, window, cols, rows, inverse, left, cross, sem_in, sem_chunk, sem_out,
):
    chunks, tile_rows, width = window.shape
    halves = (slice(0, width), slice(width, 2 * width))
    arriving = []
    for j in range(chunks):
        at = pl.ds(j * width, width)
        arriving.append(
            [
                pltpu.make_async_copy(window_hbm.at[:, at], window.at[j], sem_chunk.at[j, 0]),
                pltpu.make_async_copy(
                    cols_second_hbm.at[at], cols.at[j, :, halves[0]], sem_chunk.at[j, 1]
                ),
                pltpu.make_async_copy(
                    cols_first_hbm.at[at], cols.at[j, :, halves[1]], sem_chunk.at[j, 2]
                ),
            ]
        )
    ready = [
        pltpu.make_async_copy(rows_hbm, rows, sem_in.at[0]),
        pltpu.make_async_copy(inverse_hbm, inverse, sem_in.at[1]),
    ]
    for copy in [copy for group in arriving for copy in group] + ready:
        copy.start()
    for j in range(chunks):
        for copy in arriving[j]:
            copy.wait()
        product = dot3(split(window[j]), split(cols[j]))
        if j == 0:
            left[...] = product
        else:
            left[...] += product
    half = tile_rows // 2
    core = lax.rem(lax.axis_index("col"), 2)
    leaving = [
        pltpu.make_async_copy(
            left.at[pl.ds(pl.multiple_of(place * half, half), half)], target, sem_out.at[i]
        )
        for i, (place, target) in enumerate(((core, own_hbm), (1 - core, other_hbm)))
    ]
    for copy in leaving:
        copy.start()
    for copy in ready:
        copy.wait()
    panel = dot3(split(left[:, halves[0]]), split(inverse[...]))
    cross[...] = tdot3(split(-panel), split(rows[...]))
    leaving.append(pltpu.make_async_copy(cross, cross_hbm, sem_out.at[2]))
    leaving[-1].start()
    for copy in leaving:
        copy.wait()


def left_products(window, cols_second, cols_first, rows, inverse):
    tile_rows, tile_cols = window.shape
    width = inverse.shape[0]
    chunks = tile_cols // width
    hbm = pl.BlockSpec(memory_space=pl.ANY)
    f32 = lambda *shape: jax.ShapeDtypeStruct(shape, jnp.float32)
    buffer = lambda *shape: pltpu.VMEM(shape, jnp.float32)
    return pl.pallas_call(
        left_kernel,
        in_specs=[hbm] * 5,
        out_specs=[hbm] * 3,
        out_shape=[f32(tile_rows // 2, 2 * width)] * 2 + [f32(width, width)],
        scratch_shapes=[
            buffer(chunks, tile_rows, width),
            buffer(chunks, width, 2 * width),
            buffer(tile_rows, width),
            buffer(width, width),
            buffer(tile_rows, 2 * width),
            buffer(width, width),
            pltpu.SemaphoreType.DMA((2,)),
            pltpu.SemaphoreType.DMA((chunks, 3)),
            pltpu.SemaphoreType.DMA((3,)),
        ],
        cost_estimate=pl.CostEstimate(
            flops=12 * tile_rows * tile_cols * width,
            bytes_accessed=4 * (tile_rows * tile_cols + 2 * tile_cols * width),
            transcendentals=0,
        ),
        name="left_products",
    )(window, cols_second, cols_first, rows, inverse)


def after(value, *others):
    return lax.optimization_barrier((value,) + others)[0]


def local(
    grad_window, rows_first, cols_first, rows_second, cols_second, inverse_first, inverse_second
):
    row = lax.axis_index("row")
    col = lax.axis_index("col")
    last = 2 * SIDE - 1
    is_last = col == last
    tile_cols = grad_window.shape[1]
    width = inverse_first.shape[0]
    chunks, piece = tile_cols // width, width // SIDE
    place = place_of(row, col)

    far_place = place_of(row, col + 1)
    x, core = col // 2, col % 2

    own_left, other_left, cross = left_products(
        grad_window, cols_second, cols_first, rows_first, inverse_second
    )
    blocks = pivot_products(after(grad_window, cross), rows_second, rows_first)
    left = own_left + swap_core(other_left)

    cross = cross + lax.ppermute(cross, "col", [(2 * i, 2 * i + 1) for i in range(SIDE)])
    others = [lax.ppermute(cross, "col", [(source, last)]) for source in (3, 1, 5)]
    cross = jnp.where(is_last, cross + others[0] + others[1] + others[2], 0.0)
    late = cross.reshape(SIDE, piece, width)
    late = [block(late, (place + step) % SIDE) for step in range(SIDE)]

    def arrivals(values, swap):
        return [shift(values[step], step, swap) for step in STEPS]

    tail = cols_first[tile_cols - width :]
    held = jnp.where(is_last, tail, 0.0)
    for target in (1, 5, 3):
        held = held + lax.ppermute(after(tail, late[1]), "col", [(last, target)])

    tail = lax.ppermute(held, "col", [(2 * i + 1, 2 * i) for i in range(SIDE)])
    tail = jnp.where(core == 1, held, tail)
    left = after(left, late[1]).reshape(SIDE, -1, 2 * width)
    got_left = [shift_x(block(left, (x + step) % SIDE), step) for step in STEPS]
    left = block(left, x) + got_left[0] + got_left[1] + got_left[2]
    panel_second = matmul(-left[:, :width], inverse_second)
    panel_first = matmul(-(left[:, width:] + matmul(panel_second, tail)), inverse_first)
    panel = jnp.concatenate([panel_second, panel_first], 1)

    got = arrivals(blocks, 0)
    got_late = arrivals(late, 0)
    value = blocks[0] + got[0] + got[1] + got[2]
    late = late[0] + got_late[0] + got_late[1] + got_late[2]
    value = value.at[value.shape[0] - piece :].add(late)

    half = value.shape[0] // 2
    quarters = value.reshape(SIDE, half // 2, width)
    got = arrivals([block(quarters, (far_place + step) % SIDE) for step in range(SIDE)], 1)
    quarter = block(quarters, far_place) + got[0] + got[1] + got[2]
    inverse = jnp.where(far_place < SIDE // 2, inverse_second, inverse_first)
    quarter = matmul(-quarter, inverse)

    got = arrivals([quarter] * SIDE, 1)
    value = jnp.zeros((SIDE,) + quarter.shape, jnp.float32)
    for part, step in [(quarter, 0)] + list(zip(got, STEPS)):
        value = lax.dynamic_update_index_in_dim(value, part, (far_place - step) % SIDE, 0)
    value = value.reshape(2 * half, width)

    got = arrivals([value] * SIDE, 0)
    panel = after(panel, got[1])
    panels = jnp.zeros((SIDE,) + panel.shape, jnp.float32)
    for part, step in [(panel, 0)] + [(shift_x(panel, step), step) for step in STEPS]:
        panels = lax.dynamic_update_index_in_dim(panels, part, (x - step) % SIDE, 0)
    panels = panels.reshape(-1, 2 * width)
    both = jnp.zeros((2,) + panels.shape, jnp.float32)
    both = lax.dynamic_update_index_in_dim(both, panels, core, 0)
    both = lax.dynamic_update_index_in_dim(both, swap_core(panels), 1 - core, 0)
    both = both.reshape(-1, 2 * width)
    pivots = [jnp.zeros((chunks, SIDE, piece, width), jnp.float32)] * 2
    parts = [(value, 0)] + list(zip(got, STEPS))
    for part, step in parts:
        pivots = [
            lax.dynamic_update_index_in_dim(
                pivot, rows.reshape(chunks, piece, width), (place - step) % SIDE, 1
            )
            for pivot, rows in zip(pivots, (part[:half], part[half:]))
        ]
    both = after(both, *pivots)
    panel_second, panel_first = both[:, :width], both[:, width:]
    pivot_second, pivot_first = (pivot.reshape(tile_cols, width) for pivot in pivots)
    return (panel_second, pivot_second, panel_first, pivot_first)


def solution(mesh):
    in_specs = (
        P("row", "col"),
        P("row", None),
        P("col", None),
        P("row", None),
        P("col", None),
        P(),
        P(),
    )
    out_specs = (P("row", None), P("col", None), P("row", None), P("col", None))
    return jax.shard_map(local, mesh=mesh, in_specs=in_specs, out_specs=out_specs, check_vma=False)
```

```python
import jax
import jax.numpy as jnp
from jax import lax
from jax.experimental import pallas as pl
from jax.experimental.pallas import tpu as pltpu
from jax.sharding import PartitionSpec as P

SIDE = 4
STEPS = (2, 1, 3)


def matmul(left, right):
    return jnp.dot(left, right, precision=lax.Precision.HIGH, preferred_element_type=jnp.float32)


def pairs(step, swap):
    out = []
    for y in range(SIDE):
        for z in range(SIDE):
            for x in range(SIDE):
                for core in range(2):
                    if core == swap:
                        to_y, to_z = (y + step) % SIDE, z
                    else:
                        to_y, to_z = y, (z + step) % SIDE
                    out.append(
                        (
                            (y * SIDE + z) * 2 * SIDE + 2 * x + core,
                            (to_y * SIDE + to_z) * 2 * SIDE + 2 * x + core,
                        )
                    )
    return out


def shift(value, step, swap):
    return lax.ppermute(value, ("row", "col"), pairs(step, swap))


def shift_x(value, step):
    pairs = [(2 * x + k, 2 * ((x + step) % SIDE) + k) for x in range(SIDE) for k in range(2)]
    return lax.ppermute(value, "col", pairs)


def swap_core(value):
    return lax.ppermute(value, "col", [(i, i ^ 1) for i in range(2 * SIDE)])


def block(value, index):
    return lax.dynamic_index_in_dim(value, index, 0, keepdims=False)


def split(value):
    high = value.astype(jnp.bfloat16)
    return high, (value - high.astype(jnp.float32)).astype(jnp.bfloat16)


def dot3(left, right):
    total = jnp.dot(left[0], right[1], preferred_element_type=jnp.float32)
    total += jnp.dot(left[1], right[0], preferred_element_type=jnp.float32)
    return total + jnp.dot(left[0], right[0], preferred_element_type=jnp.float32)


def tdot3(left, right):
    def product(a, b):
        return lax.dot_general(a, b, (((0,), (0,)), ((), ())), preferred_element_type=jnp.float32)

    return product(left[0], right[1]) + product(left[1], right[0]) + product(left[0], right[0])


def place_of(row, col):
    return jnp.where(lax.rem(col, 2) == 0, lax.div(row, SIDE), lax.rem(row, SIDE))


def pivot_kernel(window_hbm, rows_second_hbm, rows_first_hbm, *refs):
    outs, refs = refs[:SIDE], refs[SIDE:]
    window, rows, pivot, high, low, sem_rows, sem_window, sem_out = refs
    chunks, _, width = window.shape
    piece = width // SIDE
    halves = (slice(0, width), slice(width, 2 * width))

    ready = [
        pltpu.make_async_copy(source, rows.at[:, halves[i]], sem_rows.at[i])
        for i, source in enumerate((rows_second_hbm, rows_first_hbm))
    ]
    arriving = [
        pltpu.make_async_copy(
            window_hbm.at[:, pl.ds(j * width, width)], window.at[j], sem_window.at[j]
        )
        for j in range(chunks)
    ]
    for copy in ready + arriving:
        copy.start()
    place = place_of(lax.axis_index("row"), lax.axis_index("col"))
    leaving = []
    for copy in ready:
        copy.wait()
    high[...], low[...] = split(rows[...])
    for j in range(chunks):
        arriving[j].wait()
        pivot[j] = tdot3(split(window[j]), (high[...], low[...]))
        for step in range(SIDE):
            start = pl.multiple_of(lax.rem(place + step, SIDE) * piece, piece)
            for i in range(2):
                copy = pltpu.make_async_copy(
                    pivot.at[j, pl.ds(start, piece), halves[i]],
                    outs[step].at[pl.ds((i * chunks + j) * piece, piece)],
                    sem_out.at[j, i * SIDE + step],
                )
                copy.start()
                leaving.append(copy)
    for copy in leaving:
        copy.wait()


def pivot_products(window, rows_second, rows_first):
    tile_rows, tile_cols = window.shape
    width = rows_first.shape[1]
    chunks = tile_cols // width
    hbm = pl.BlockSpec(memory_space=pl.ANY)
    buffer = lambda *shape: pltpu.VMEM(shape, jnp.float32)
    return pl.pallas_call(
        pivot_kernel,
        in_specs=[hbm] * 3,
        out_specs=[hbm] * SIDE,
        out_shape=[jax.ShapeDtypeStruct((2 * tile_cols // SIDE, width), jnp.float32)] * SIDE,
        scratch_shapes=[
            buffer(chunks, tile_rows, width),
            buffer(tile_rows, 2 * width),
            buffer(chunks, width, 2 * width),
            pltpu.VMEM((tile_rows, 2 * width), jnp.bfloat16),
            pltpu.VMEM((tile_rows, 2 * width), jnp.bfloat16),
            pltpu.SemaphoreType.DMA((2,)),
            pltpu.SemaphoreType.DMA((chunks,)),
            pltpu.SemaphoreType.DMA((chunks, 2 * SIDE)),
        ],
        cost_estimate=pl.CostEstimate(
            flops=12 * tile_rows * tile_cols * width,
            bytes_accessed=4 * (tile_rows * tile_cols + 2 * tile_cols * width),
            transcendentals=0,
        ),
        name="pivot_products",
    )(window, rows_second, rows_first)


def left_kernel(
    window_hbm, cols_second_hbm, cols_first_hbm, rows_hbm, inverse_hbm, own_hbm, other_hbm,
    cross_hbm, window, cols, rows, inverse, left, cross, sem_in, sem_chunk, sem_out,
):
    chunks, tile_rows, width = window.shape
    halves = (slice(0, width), slice(width, 2 * width))
    arriving = []
    for j in range(chunks):
        at = pl.ds(j * width, width)
        arriving.append(
            [
                pltpu.make_async_copy(window_hbm.at[:, at], window.at[j], sem_chunk.at[j, 0]),
                pltpu.make_async_copy(
                    cols_second_hbm.at[at], cols.at[j, :, halves[0]], sem_chunk.at[j, 1]
                ),
                pltpu.make_async_copy(
                    cols_first_hbm.at[at], cols.at[j, :, halves[1]], sem_chunk.at[j, 2]
                ),
            ]
        )
    ready = [
        pltpu.make_async_copy(rows_hbm, rows, sem_in.at[0]),
        pltpu.make_async_copy(inverse_hbm, inverse, sem_in.at[1]),
    ]
    for copy in [copy for group in arriving for copy in group] + ready:
        copy.start()
    for j in range(chunks):
        for copy in arriving[j]:
            copy.wait()
        product = dot3(split(window[j]), split(cols[j]))
        if j == 0:
            left[...] = product
        else:
            left[...] += product
    half = tile_rows // 2
    core = lax.rem(lax.axis_index("col"), 2)
    leaving = [
        pltpu.make_async_copy(
            left.at[pl.ds(pl.multiple_of(place * half, half), half)], target, sem_out.at[i]
        )
        for i, (place, target) in enumerate(((core, own_hbm), (1 - core, other_hbm)))
    ]
    for copy in leaving:
        copy.start()
    for copy in ready:
        copy.wait()
    panel = dot3(split(left[:, halves[0]]), split(inverse[...]))
    cross[...] = tdot3(split(-panel), split(rows[...]))
    leaving.append(pltpu.make_async_copy(cross, cross_hbm, sem_out.at[2]))
    leaving[-1].start()
    for copy in leaving:
        copy.wait()


def left_products(window, cols_second, cols_first, rows, inverse):
    tile_rows, tile_cols = window.shape
    width = inverse.shape[0]
    chunks = tile_cols // width
    hbm = pl.BlockSpec(memory_space=pl.ANY)
    f32 = lambda *shape: jax.ShapeDtypeStruct(shape, jnp.float32)
    buffer = lambda *shape: pltpu.VMEM(shape, jnp.float32)
    return pl.pallas_call(
        left_kernel,
        in_specs=[hbm] * 5,
        out_specs=[hbm] * 3,
        out_shape=[f32(tile_rows // 2, 2 * width)] * 2 + [f32(width, width)],
        scratch_shapes=[
            buffer(chunks, tile_rows, width),
            buffer(chunks, width, 2 * width),
            buffer(tile_rows, width),
            buffer(width, width),
            buffer(tile_rows, 2 * width),
            buffer(width, width),
            pltpu.SemaphoreType.DMA((2,)),
            pltpu.SemaphoreType.DMA((chunks, 3)),
            pltpu.SemaphoreType.DMA((3,)),
        ],
        cost_estimate=pl.CostEstimate(
            flops=12 * tile_rows * tile_cols * width,
            bytes_accessed=4 * (tile_rows * tile_cols + 2 * tile_cols * width),
            transcendentals=0,
        ),
        name="left_products",
    )(window, cols_second, cols_first, rows, inverse)


def after(value, *others):
    return lax.optimization_barrier((value,) + others)[0]


def local(
    grad_window, rows_first, cols_first, rows_second, cols_second, inverse_first, inverse_second
):
    row = lax.axis_index("row")
    col = lax.axis_index("col")
    last = 2 * SIDE - 1
    is_last = col == last
    tile_cols = grad_window.shape[1]
    width = inverse_first.shape[0]
    chunks, piece = tile_cols // width, width // SIDE
    place = place_of(row, col)

    far_place = place_of(row, col + 1)
    x, core = col // 2, col % 2

    own_left, other_left, cross = left_products(
        grad_window, cols_second, cols_first, rows_first, inverse_second
    )
    blocks = pivot_products(after(grad_window, cross), rows_second, rows_first)
    left = own_left + swap_core(other_left)

    cross = cross + swap_core(cross)
    others = [lax.ppermute(cross, "col", [(source, last)]) for source in (3, 1, 5)]
    cross = jnp.where(is_last, cross + others[0] + others[1] + others[2], 0.0)
    late = cross.reshape(SIDE, piece, width)
    late = [block(late, (place + step) % SIDE) for step in range(SIDE)]

    def arrivals(values, swap):
        return [shift(values[step], step, swap) for step in STEPS]

    tail = cols_first[tile_cols - width :]
    held = jnp.where(is_last, tail, 0.0)
    for target in (1, 5, 3):
        held = held + lax.ppermute(after(tail, late[1]), "col", [(last, target)])

    tail = lax.ppermute(held, "col", [(2 * i + 1, 2 * i) for i in range(SIDE)])
    tail = jnp.where(core == 1, held, tail)
    left = after(left, late[1]).reshape(SIDE, -1, 2 * width)
    got_left = [shift_x(block(left, (x + step) % SIDE), step) for step in STEPS]
    left = block(left, x) + got_left[0] + got_left[1] + got_left[2]
    panel_second = matmul(-left[:, :width], inverse_second)
    panel_first = matmul(-(left[:, width:] + matmul(panel_second, tail)), inverse_first)
    panel = jnp.concatenate([panel_second, panel_first], 1)

    got = arrivals(blocks, 0)
    got_late = arrivals(late, 0)
    value = blocks[0] + got[0] + got[1] + got[2]
    late = late[0] + got_late[0] + got_late[1] + got_late[2]
    value = value.at[value.shape[0] - piece :].add(late)

    half = value.shape[0] // 2
    quarters = value.reshape(SIDE, half // 2, width)
    got = arrivals([block(quarters, (far_place + step) % SIDE) for step in range(SIDE)], 1)
    quarter = block(quarters, far_place) + got[0] + got[1] + got[2]
    inverse = jnp.where(far_place < SIDE // 2, inverse_second, inverse_first)
    quarter = matmul(-quarter, inverse)

    got = arrivals([quarter] * SIDE, 1)
    value = jnp.zeros((SIDE,) + quarter.shape, jnp.float32)
    for part, step in [(quarter, 0)] + list(zip(got, STEPS)):
        value = lax.dynamic_update_index_in_dim(value, part, (far_place - step) % SIDE, 0)
    value = value.reshape(2 * half, width)

    got = arrivals([value] * SIDE, 0)
    panel = after(panel, got[1])
    panels = jnp.zeros((SIDE,) + panel.shape, jnp.float32)
    for part, step in [(panel, 0)] + [(shift_x(panel, step), step) for step in STEPS]:
        panels = lax.dynamic_update_index_in_dim(panels, part, (x - step) % SIDE, 0)
    panels = panels.reshape(-1, 2 * width)
    both = jnp.zeros((2,) + panels.shape, jnp.float32)
    both = lax.dynamic_update_index_in_dim(both, panels, core, 0)
    both = lax.dynamic_update_index_in_dim(both, swap_core(panels), 1 - core, 0)
    both = both.reshape(-1, 2 * width)
    pivots = [jnp.zeros((chunks, SIDE, piece, width), jnp.float32)] * 2
    parts = [(value, 0)] + list(zip(got, STEPS))
    for part, step in parts:
        pivots = [
            lax.dynamic_update_index_in_dim(
                pivot, rows.reshape(chunks, piece, width), (place - step) % SIDE, 1
            )
            for pivot, rows in zip(pivots, (part[:half], part[half:]))
        ]
    both = after(both, *pivots)
    panel_second, panel_first = both[:, :width], both[:, width:]
    pivot_second, pivot_first = (pivot.reshape(tile_cols, width) for pivot in pivots)
    return (panel_second, pivot_second, panel_first, pivot_first)


def solution(mesh):
    in_specs = (
        P("row", "col"),
        P("row", None),
        P("col", None),
        P("row", None),
        P("col", None),
        P(),
        P(),
    )
    out_specs = (P("row", None), P("col", None), P("row", None), P("col", None))
    return jax.shard_map(local, mesh=mesh, in_specs=in_specs, out_specs=out_specs, check_vma=False)
```
